512 devices in a mesh: row: 16 (over x_hi, y), col: 32 (over z, x_lo, core).
Axes of the slice: x: 4 (x_hi: 2, x_lo: 2; x = x_hi * 2 + x_lo), y: 8, z: 8, core: 2. Of those that a mesh axis runs over, the one named last changes fastest.
Arguments:
- operator: float32 [4096, 4096], P('row', 'col'), may hold values from -0.09375 to 0.09375
- state: float32 [4096, 4096], P('row', 'col'), may hold values from -60 to 60, as said below
- source: float32 [4096, 4096], P('row', 'col'), may hold values from -60 to 60, as said below
Outputs:
- state_next: float32 [4096, 4096], P('row', 'col')
- operator_fourth: float32 [4096, 4096], P('row', 'col')
The draws below stay inside these ranges and needn't reach their ends.
Inputs may be any that keep to these rules, and one draw needn't show every extreme that they name: symmetric: state equals its transpose. symmetric: source equals its transpose.
All inputs are finite; a program needn't handle non-finite values.
Results may differ from the reference program's by a relative error of at most 0.000098.
Values sent between devices are 32-bit elements; how exact they have to be, the bound alone decides.
A program may use at most 64 MiB of HBM per device.

```python
import jax
import jax.numpy as jnp
from jax import lax

N = 4096


def symmetric_draw(key):
    base = jax.random.truncated_normal(key, -6.0, 6.0, (N, N), jnp.float32)
    return ((base + base.T) * 0.5).astype(jnp.float32)


def draw_state(key, part):
    return symmetric_draw(jax.random.fold_in(key, 11))


def draw_source(key, part):
    return symmetric_draw(jax.random.fold_in(key, 23))


def levels(key, shape, shards, low, top_value):
    factor_of, own = 1.0, jax.random.fold_in(key, 6)
    for axis_at, blocks in shards:
        steps = jnp.exp(jax.random.uniform(jax.random.fold_in(own, axis_at), (blocks,), jnp.float32, low / len(shards), top_value / len(shards)))
        factor_of = factor_of * jnp.repeat(steps, shape[axis_at] // blocks).reshape([-1 if axis == axis_at else 1 for axis in range(len(shape))])
    return factor_of


def gaussian(key, shape, deviation, bound, pieces=(), held_as=jnp.bfloat16):
    entries = jax.random.normal(key, shape, jnp.float32) * deviation
    if len(pieces) > 0:
        entries = levels(key, shape, pieces, -0.22, 0.18) * entries
    return jnp.clip(entries, min=-bound, max=bound).astype(held_as)


def setup_inputs(seed: int = 0) -> dict:
    streams_of = jax.random.split(jax.random.key(seed), 4)
    return {
        "operator": gaussian(streams_of[0], (N, N), N ** -0.5, 0.09375, ((0, 16), (1, 32)), jnp.float32),
        "state": draw_state(jax.random.fold_in(streams_of[3], 71), 0),
        "source": draw_source(jax.random.fold_in(streams_of[3], 71), 0),
    }


def matmul(left, right):
    return jnp.dot(left, right, preferred_element_type=jnp.float32, precision=lax.Precision.HIGHEST)


def reference(operator, state, source):
    product = matmul(operator, state)
    square = matmul(operator, operator)
    state_next = matmul(operator, product.T) + source
    operator_fourth = matmul(square, square)
    return state_next, operator_fourth
```

```python
import functools
import itertools

import jax
import jax.numpy as jnp
from jax import lax
from jax.experimental import pallas as pl
from jax.experimental.pallas import tpu as pltpu
from jax.sharding import PartitionSpec as P

MESH = pl.DeviceIdType.MESH
B, H = 256, 128
RINGS = ((0, 0), (0, 1), (1, 0), (1, 1))
BF, F32 = jnp.bfloat16, jnp.float32
COPIES = 130


def length(g, d):
    return 4 if g == d else 3


def sign(d):
    return 1 if d == 0 else -1


def wrap(v):
    return lax.rem(v + 16, 8)


def halves(v):
    hi = v.astype(BF)
    return hi, (v - hi.astype(F32)).astype(BF)


def dot(a, b):
    return jnp.dot(a, b, preferred_element_type=F32)


def dot_t(a, b):
    return lax.dot_general(a, b, (((1,), (1,)), ((), ())), preferred_element_type=F32)


def kernel(a_ref, x_ref, q_ref, n_ref, f_ref, ar, ac, xc, sr, sc, part, swap, run, last, s_own, t_own, acc2, acc1, p2, send, recv):
    row, col = lax.axis_index("row"), lax.axis_index("col")
    xh, y = row // 8, lax.rem(row, 8)
    z, xl, core = col // 4, lax.rem(col // 2, 2), lax.rem(col, 2)
    ids = itertools.count()
    sent = []

    y_dev = [(xh * 8 + wrap(y + sign(d)), col) for d in (0, 1)]
    z_dev = [(row, wrap(z + sign(d)) * 4 + xl * 2 + core) for d in (0, 1)]
    hi_dev = ((1 - xh) * 8 + y, col)
    lo_dev = (row, z * 4 + (1 - xl) * 2 + core)
    mate = (row, z * 4 + xl * 2 + (1 - core))

    barrier = pltpu.get_barrier_semaphore()
    greeted = (*y_dev, *z_dev, hi_dev, lo_dev, mate)
    for device in greeted:
        pl.semaphore_signal(barrier, inc=1, device_id=device, device_id_type=MESH)
    pl.semaphore_wait(barrier, len(greeted))

    def copy(k, src, dst, device):
        return pltpu.make_async_remote_copy(
            src_ref=src, dst_ref=dst, send_sem=send.at[k], recv_sem=recv.at[k], device_id=device, device_id_type=MESH
        )

    def start(k, src, dst, device):
        c = copy(k, src, dst, device)
        c.start()
        sent.append(c)

    def arrived(k, dst):
        copy(k, dst, dst, mate).wait_recv()

    class Panel:
        def __init__(self, buf, own, at, pos, devices, partner, mated):
            self.buf, self.own, self.at, self.pos = buf, own, at, pos
            self.devices, self.partner, self.mated = devices, partner, mated
            self.kx = next(ids)
            self.k = {(g, d, s): next(ids) for g, d in RINGS for s in range(1, length(g, d) + 1)}
            self.km = {e: next(ids) for e in ("own", "x", *self.k)} if mated else {}

        def slot(self, g, p, other=False):
            return self.buf.at[self.at(g, p, other)]

        def place(self, g, d, s):
            return g, wrap(self.pos - sign(d) * s)

        def where(self, e):
            if e == "own":
                return 0, self.pos
            return (1, self.pos) if e == "x" else self.place(*e)

        def to_mate(self, e):
            if self.mated:
                here = self.slot(*self.where(e))
                start(self.km[e], self.own if e == "own" else here, here, mate)

        def from_mate(self):
            for e, k in self.km.items():
                arrived(k, self.slot(*self.where(e), True))

        def exchange(self):
            start(self.kx, self.own, self.slot(0, self.pos), self.partner)

        def launch(self):
            for d in (0, 1):
                self.forward(0, d, 1)
            self.to_mate("own")

        def relaunch(self):
            arrived(self.kx, self.slot(1, self.pos))
            for d in (0, 1):
                self.forward(1, d, 1)
            self.to_mate("x")

        def forward(self, g, d, s):
            there = self.slot(*self.place(g, d, s - 1))
            start(self.k[g, d, s], self.own if g == 0 and s == 1 else there, there, self.devices[d])

        def step(self, s):
            for g, d in RINGS:
                if s <= length(g, d):
                    arrived(self.k[g, d, s], self.slot(*self.place(g, d, s)))
                    if s < length(g, d):
                        self.forward(g, d, s + 1)
                    self.to_mate((g, d, s))

    def row_at(g, p, other):
        lo = xl if g == 0 else 1 - xl
        c = 1 - core if other else core
        return p * 4 + lo * 2 + c

    def col_at(g, p, other):
        return (xh if g == 0 else 1 - xh) * 8 + p

    def row_panel(buf, own):
        return Panel(buf, own, row_at, z, z_dev, lo_dev, True)

    def col_panel(buf, own):
        return Panel(buf, own, col_at, y, y_dev, hi_dev, False)

    def multiply(left, right, out):
        acc2[...] = jnp.zeros_like(acc2)
        acc1[...] = jnp.zeros_like(acc1)

        def body(i, carry):
            lh, ll = halves(jnp.concatenate([left[4 * i + j] for j in range(4)], axis=1))
            rh, rl = halves(jnp.concatenate([right[2 * i + j] for j in range(2)], axis=0))
            acc2[...] += dot(lh, jnp.concatenate([rh, rl], axis=1))
            acc1[...] += dot(ll, rh)
            return carry

        lax.fori_loop(0, 8, body, 0)
        out[...] = acc2[:, :H] + acc2[:, H:] + acc1[...]

    a_row, a_col, x_col = row_panel(ar, a_ref), col_panel(ac, a_ref), col_panel(xc, x_ref)
    s_row, s_col = row_panel(sr, s_own), col_panel(sc, s_own)

    a_col.launch()
    a_row.launch()
    a_col.exchange()
    a_row.exchange()
    x_col.exchange()
    ac[row] = a_ref[...]
    ar[col] = a_ref[...]
    xc[row] = x_ref[...]
    a_col.relaunch()
    a_row.relaunch()
    for s in range(1, 5):
        a_col.step(s)
        a_row.step(s)
        if s == 3:
            x_col.launch()
    x_col.relaunch()
    a_row.from_mate()
    multiply(ar, ac, s_own)
    s_row.exchange()
    s_row.launch()
    s_col.exchange()
    sr[col] = s_own[...]
    sc[row] = s_own[...]
    x_col.step(1)
    s_row.relaunch()
    for s in range(1, 5):
        if s > 1:
            x_col.step(s)
        s_row.step(s)
        if s == 3:
            s_col.launch()
    s_col.relaunch()
    multiply(ar, xc, t_own)

    hi, lo = halves(t_own[...])
    p2[...] = jnp.concatenate([hi, lo], axis=1)
    order = (4, 3, 5, 2, 6, 1, 7, 0)
    kn = {o: next(ids) for o in order}

    def part_of(o):
        zz = wrap(z + o)
        for l in (0, 1):
            bh, bl = halves(ac[2 * zz + l])
            both = dot_t(p2[...], jnp.concatenate([bh, bh], axis=1)) + dot_t(p2[:, :H], bl)
            part[0, zz, l] = both[:, :H]
            part[1, zz, l] = both[:, H:]
        start(kn[o], part.at[1 - core, zz], swap.at[zz], mate)

    for o in order:
        part_of(o)

    kr = {(g, d, s): next(ids) for g, d in RINGS for s in range(1, length(g, d) + 1)}
    at_run = {e: i for i, e in enumerate(kr)}
    have = set()

    def share(g, off):
        zz = wrap(z + off)
        if off % 8 not in have:
            have.add(off % 8)
            arrived(kn[off % 8], swap.at[zz])
        l = xl if g == 0 else 1 - xl
        return part[core, zz, l] + swap[zz, l]

    for g, d in reversed(RINGS):
        off = sign(d) * length(g, d)
        l = xl if g == 0 else 1 - xl
        zz = wrap(z + off)
        part[core, zz, l] = share(g, off)
        start(kr[g, d, 1], part.at[core, zz, l], run.at[at_run[g, d, 1]], z_dev[d])

    for s in range(1, 5):
        s_col.step(s)
        for g, d in reversed(RINGS):
            if s < length(g, d):
                here = run.at[at_run[g, d, s]]
                arrived(kr[g, d, s], here)
                here[...] += share(g, sign(d) * (length(g, d) - s))
                start(kr[g, d, s + 1], here, run.at[at_run[g, d, s + 1]], z_dev[d])

    def total(g):
        both = [run.at[at_run[g, d, length(g, d)]] for d in (0, 1)]
        for d in (0, 1):
            arrived(kr[g, d, length(g, d)], both[d])
        return both[0][...] + both[1][...] + share(g, 0)

    k_last = next(ids)
    t_own[...] = total(1)
    start(k_last, t_own, last, lo_dev)
    n_ref[...] = total(0) + q_ref[...]
    s_row.from_mate()
    multiply(sr, sc, f_ref)
    arrived(k_last, last)
    n_ref[...] += last[...]
    for c in sent:
        c.wait_send()
    assert next(ids) == COPIES


def on_device(operator, state, source):
    block = jax.ShapeDtypeStruct((B, H), F32)
    vmem = pl.BlockSpec(memory_space=pltpu.VMEM)

    def blocks(*lead):
        return pltpu.VMEM((*lead, B, H), F32)

    return pl.pallas_call(
        kernel,
        out_shape=(block, block),
        in_specs=[vmem] * 3,
        out_specs=(vmem, vmem),
        scratch_shapes=[
            blocks(32),
            blocks(16),
            blocks(16),
            blocks(32),
            blocks(16),
            blocks(2, 8, 2),
            blocks(8, 2),
            blocks(14),
            blocks(),
            blocks(),
            blocks(),
            pltpu.VMEM((B, B), F32),
            blocks(),
            pltpu.VMEM((B, B), BF),
            pltpu.SemaphoreType.DMA((COPIES,)),
            pltpu.SemaphoreType.DMA((COPIES,)),
        ],
        compiler_params=pltpu.CompilerParams(collective_id=0, has_side_effects=True, vmem_limit_bytes=56 << 20),
        name="smith",
    )(operator, state, source)


def solution(mesh):
    spec = P("row", "col")
    return jax.shard_map(on_device, mesh=mesh, in_specs=(spec, spec, spec), out_specs=(spec, spec), check_vma=False)
```

```python
import functools
import itertools

import jax
import jax.numpy as jnp
from jax import lax
from jax.experimental import pallas as pl
from jax.experimental.pallas import tpu as pltpu
from jax.sharding import PartitionSpec as P

MESH = pl.DeviceIdType.MESH
B, H = 256, 128
RINGS = ((0, 0), (0, 1), (1, 0), (1, 1))
BF, F32 = jnp.bfloat16, jnp.float32
PARTS = 2
SHORT = {"a_row": (4, 4), "a_col": (4, 4), "x_col": (4, 4), "s_row": (2, 2), "s_col": (4, 4), "sum": (4, 4)}


def reach(d, p):
    return 4 if d == p else 3


def hops(short, g, d, p):
    return min(short[d == p], reach(d, p)) if g else reach(d, p)


def events(short):
    return [(g, d, s, p) for g, d in RINGS for p in range(PARTS) for s in range(1, hops(short, g, d, p) + 1)]


def far(short):
    return [(d, s, p) for s in range(1, 5) for d in (0, 1) for p in range(PARTS) if hops(short, 1, d, p) < s <= reach(d, p)]


def sign(d):
    return 1 if d == 0 else -1


def wrap(v):
    return lax.rem(v + 16, 8)


def copies():
    count = {name: len(events(short)) + len(far(short)) for name, short in SHORT.items()}
    return sum(count.values()) + 5 * PARTS + 2 + 8 + 1


def piece(ref, p):
    return ref.at[pl.ds(p * (B // PARTS), B // PARTS)]


def halves(v):
    hi = v.astype(BF)
    return hi, (v - hi.astype(F32)).astype(BF)


def dot(a, b):
    return jnp.dot(a, b, preferred_element_type=F32)


def dot_t(a, b):
    return lax.dot_general(a, b, (((1,), (1,)), ((), ())), preferred_element_type=F32)


def kernel(a_ref, x_ref, q_ref, n_ref, f_ref, ar, ac, xc, sr, sc, part, swap, run, loan, last, s_own, t_own, acc2, acc1, p2, send, recv):
    row, col = lax.axis_index("row"), lax.axis_index("col")
    xh, y = row // 8, lax.rem(row, 8)
    z, xl, core = col // 4, lax.rem(col // 2, 2), lax.rem(col, 2)
    ids, groups = itertools.count(), itertools.count()

    y_dev = [(xh * 8 + wrap(y + sign(d)), col) for d in (0, 1)]
    z_dev = [(row, wrap(z + sign(d)) * 4 + xl * 2 + core) for d in (0, 1)]
    hi_dev = ((1 - xh) * 8 + y, col)
    lo_dev = (row, z * 4 + (1 - xl) * 2 + core)
    mate = (row, z * 4 + xl * 2 + (1 - core))

    barrier = pltpu.get_barrier_semaphore()
    across = [(row, wrap(z + sign(d)) * 4 + (1 - xl) * 2 + core) for d in (0, 1)]
    greeted = (*y_dev, *z_dev, *across, hi_dev, lo_dev, mate)
    for device in greeted:
        pl.semaphore_signal(barrier, inc=1, device_id=device, device_id_type=MESH)
    pl.semaphore_wait(barrier, len(greeted))

    def copy(k, src, dst, device, group=0):
        return pltpu.make_async_remote_copy(
            src_ref=src, dst_ref=dst, send_sem=send.at[group], recv_sem=recv.at[k], device_id=device, device_id_type=MESH
        )

    def start(group, k, src, dst, device):
        copy(k, src, dst, device, group).start()

    def arrived(k, dst):
        copy(k, dst, dst, mate).wait_recv()

    def all_sent(group, as_much):
        copy(0, as_much, as_much, mate, group).wait_send()

    class Panel:
        def __init__(self, buf, own, at, pos, devices, partner, mated, short):
            self.buf, self.own, self.at, self.pos = buf, own, at, pos
            self.devices, self.partner, self.mated, self.short = devices, partner, mated, short
            self.kx = [next(ids) for _ in range(PARTS)]
            self.group = next(groups)
            self.k = {e: next(ids) for e in events(short)}
            self.kf = {e: next(ids) for e in far(short)}
            self.km = next(ids) if mated else None

        def slot(self, g, d, s, p):
            return piece(self.buf.at[self.at(g, wrap(self.pos - sign(d) * s))], p)

        def to_mate(self, e, src=None):
            if self.mated:
                here = self.slot(*e)
                start(self.group, self.km, here if src is None else src, here, mate)

        def from_mate(self):
            arrived(self.km, self.buf.at[pl.ds(0, 16)])

        def all_sent(self):
            all_sent(self.group, self.buf.at[pl.ds(0, 31 if self.mated else 15)])

        def exchange(self):
            for p in range(PARTS):
                start(self.group, self.kx[p], piece(self.own, p), self.slot(0, 0, 0, p), self.partner)

        def forward(self, g, d, s, p):
            there = self.slot(g, d, s - 1, p)
            start(self.group, self.k[g, d, s, p], piece(self.own, p) if g == 0 and s == 1 else there, there, self.devices[d])

        def launch(self):
            for p in range(PARTS):
                for d in (0, 1):
                    self.forward(0, d, 1, p)
            for p in range(PARTS):
                self.to_mate((0, 0, 0, p), piece(self.own, p))

        def relaunch(self, p):
            arrived(self.kx[p], self.slot(1, 0, 0, p))
            for d in (0, 1):
                if hops(self.short, 1, d, p):
                    self.forward(1, d, 1, p)
            self.to_mate((1, 0, 0, p))

        def hop(self, g, d, s, p):
            e = (g, d, s, p)
            if e not in self.k:
                return
            here = self.slot(*e)
            arrived(self.k[e], here)
            if (g, d, s + 1, p) in self.k:
                self.forward(g, d, s + 1, p)
            if g == 0 and e[1:] in self.kf:
                start(self.group, self.kf[e[1:]], here, here, self.partner)
            self.to_mate(e)

        def step(self, s, g, p):
            if s == 1 and g == 0:
                self.relaunch(p)
            for d in (0, 1):
                self.hop(g, d, s, p)

        def finish(self, steps=(1, 2, 3, 4)):
            for e, k in self.kf.items():
                if e[1] in steps:
                    arrived(k, self.slot(1, *e))
                    self.to_mate((1, *e))

    def step(s, *panels):
        for g in (0, 1):
            for p in range(PARTS):
                for panel in panels:
                    panel.step(s, g, p)

    def row_at(g, p):
        lo = xl if g == 0 else 1 - xl
        return p * 4 + lo * 2 + core

    def col_at(g, p):
        return (xh if g == 0 else 1 - xh) * 8 + p

    def row_panel(buf, own, short):
        return Panel(buf, own, row_at, z, z_dev, lo_dev, True, short)

    def col_panel(buf, own, short):
        return Panel(buf, own, col_at, y, y_dev, hi_dev, False, short)

    def clear():
        acc2[...] = jnp.zeros_like(acc2)
        acc1[...] = jnp.zeros_like(acc1)

    def terms(left, right, first, count):
        def body(i, carry):
            here = wrap(y + i + first)
            lh, ll = halves(jnp.concatenate([left[2 * here + j] for j in (0, 1, 16, 17)], axis=1))
            rh, rl = halves(jnp.concatenate([right[here + j] for j in (0, 8)], axis=0))
            acc2[...] += dot(lh, jnp.concatenate([rh, rl], axis=1))
            acc1[...] += dot(ll, rh)
            return carry

        lax.fori_loop(0, count, body, 0)

    def value():
        return acc2[:, :H] + acc2[:, H:] + acc1[...]

    a_row, a_col = row_panel(ar, a_ref, SHORT["a_row"]), col_panel(ac, a_ref, SHORT["a_col"])
    s_row, s_col = row_panel(sr, s_own, SHORT["s_row"]), col_panel(sc, s_own, SHORT["s_col"])
    x_col = col_panel(xc, x_ref, SHORT["x_col"])

    a_col.launch()
    a_row.launch()
    a_col.exchange()
    a_row.exchange()
    ac[row] = a_ref[...]
    ar[col] = a_ref[...]
    xc[row] = x_ref[...]
    for s in range(1, 5):
        step(s, a_col, a_row)
        if s == 2:
            x_col.exchange()
        if s == 3:
            x_col.launch()
    a_row.finish()
    a_col.finish()
    a_row.from_mate()
    clear()
    terms(ar, ac, 0, 8)
    s_own[...] = value()
    s_row.launch()
    s_row.exchange()
    s_col.exchange()
    sr[col] = s_own[...]
    sc[row] = s_own[...]
    for s in range(1, 5):
        step(s, x_col, s_row)
        if s == 3:
            s_col.launch()
            clear()
            terms(ar, xc, -3, 7)
    x_col.finish()
    terms(ar, xc, 4, 1)
    t_own[...] = value()

    hi, lo = halves(t_own[...])
    p2[...] = jnp.concatenate([hi, lo], axis=1)
    order = (4, 3, 5, 2, 6, 1, 7, 0)
    kn = {o: next(ids) for o in order}
    g_part, g_sum = next(groups), next(groups)

    def part_of(o):
        zz = wrap(z + o)
        for l in (0, 1):
            bh, bl = halves(ac[2 * zz + l])
            both = dot_t(p2[...], jnp.concatenate([bh, bh], axis=1)) + dot_t(p2[:, :H], bl)
            part[0, zz, l] = both[:, :H]
            part[1, zz, l] = both[:, H:]
        start(g_part, kn[o], part.at[1 - core, zz], swap.at[zz], mate)

    short = SHORT["sum"]
    runs, lent = events(short), far(short)
    kr = {e: next(ids) for e in runs}
    kl = {e: next(ids) for e in lent}
    have = set()

    def share(g, d, s, p):
        zz = wrap(z + sign(d) * s)
        o = sign(d) * s % 8
        if o not in have:
            have.add(o)
            arrived(kn[o], swap.at[zz])
        l = xl if g == 0 else 1 - xl
        return piece(part.at[core, zz, l], p), piece(swap.at[zz, l], p)

    def lend(d, s, p):
        mine, theirs = share(1, d, s, p)
        mine[...] += theirs[...]
        start(g_sum, kl[d, s, p], mine, loan.at[lent.index((d, s, p))], lo_dev)

    def added(value, g, d, s, p):
        mine, theirs = share(g, d, s, p)
        value = mine[...] + theirs[...] if value is None else value + (mine[...] + theirs[...])
        if g == 0 and (d, s, p) in kl:
            here = loan.at[lent.index((d, s, p))]
            arrived(kl[d, s, p], here)
            value = value + here[...]
        return value

    def relay(g, d, p, s):
        n = hops(short, g, d, p)
        if not 1 <= s <= n:
            return
        if s == n:
            here = share(g, d, s, p)[0]
            here[...] = added(None, g, d, s, p)
        else:
            e = (g, d, n - s, p)
            here = run.at[runs.index(e)]
            arrived(kr[e], here)
            here[...] = added(here[...], g, d, s, p)
        e = (g, d, n - s + 1, p)
        there = across[d] if g == 1 and s == 1 else z_dev[d]
        start(g_sum, kr[e], here, run.at[runs.index(e)], there)

    for o in order[:3]:
        part_of(o)
    for d, s, p in reversed(lent):
        lend(d, s, p)
    for o in order[3:]:
        part_of(o)

    def relays(g, back):
        for p in range(PARTS):
            for d in (0, 1):
                relay(g, d, p, hops(short, g, d, p) - back)

    k_last = next(ids)
    relays(1, 0)
    relays(0, 0)
    for p in range(PARTS):
        mine, theirs = share(1, 0, 0, p)
        mine[...] += theirs[...]
    start(g_sum, k_last, part.at[core, z, 1 - xl], last, lo_dev)
    for back in range(1, 4):
        for g in (1, 0):
            for p in range(PARTS):
                s_col.step(back, 1 - g, p)
                for d in (0, 1):
                    relay(g, d, p, hops(short, g, d, p) - back)
        if back == 2:
            s_row.finish()
            s_row.from_mate()
    clear()
    terms(sr, sc, -3, 7)
    step(4, s_col)
    s_col.finish()
    terms(sr, sc, 4, 1)
    f_ref[...] = value()
    arrived(k_last, last)
    n_ref[...] = q_ref[...] + last[...]
    for p in range(PARTS):
        here = piece(n_ref, p)
        here[...] = added(here[...], 0, 0, 0, p)
        for g in (1, 0):
            for d in (0, 1):
                e = (g, d, hops(short, g, d, p), p)
                arrived(kr[e], run.at[runs.index(e)])
                here[...] += run[runs.index(e)]
    for panel in (a_row, a_col, x_col, s_row, s_col):
        panel.all_sent()
    all_sent(g_part, swap.at[...])
    all_sent(g_sum, ar.at[pl.ds(0, 15)])
    assert next(ids) == copies()


def on_device(operator, state, source):
    block = jax.ShapeDtypeStruct((B, H), F32)
    vmem = pl.BlockSpec(memory_space=pltpu.VMEM)

    def blocks(*lead):
        return pltpu.VMEM((*lead, B, H), F32)

    return pl.pallas_call(
        kernel,
        out_shape=(block, block),
        in_specs=[vmem] * 3,
        out_specs=(vmem, vmem),
        scratch_shapes=[
            blocks(32),
            blocks(16),
            blocks(16),
            blocks(32),
            blocks(16),
            blocks(2, 8, 2),
            blocks(8, 2),
            pltpu.VMEM((len(events(SHORT["sum"])), B // PARTS, H), F32),
            pltpu.VMEM((max(1, len(far(SHORT["sum"]))), B // PARTS, H), F32),
            blocks(),
            blocks(),
            blocks(),
            pltpu.VMEM((B, B), F32),
            blocks(),
            pltpu.VMEM((B, B), BF),
            pltpu.SemaphoreType.DMA((7,)),
            pltpu.SemaphoreType.DMA((copies(),)),
        ],
        compiler_params=pltpu.CompilerParams(collective_id=0, has_side_effects=True, vmem_limit_bytes=56 << 20),
        name="smith",
    )(operator, state, source)


def solution(mesh):
    spec = P("row", "col")
    return jax.shard_map(on_device, mesh=mesh, in_specs=(spec, spec, spec), out_specs=(spec, spec), check_vma=False)
```

```python
import functools
import itertools

import jax
import jax.numpy as jnp
from jax import lax
from jax.experimental import pallas as pl
from jax.experimental.pallas import tpu as pltpu
from jax.sharding import PartitionSpec as P

MESH = pl.DeviceIdType.MESH
B, H = 256, 128
RINGS = ((0, 0), (0, 1), (1, 0), (1, 1))
BF, F32 = jnp.bfloat16, jnp.float32
PARTS = 2
ORDER = (
    "begin",
    "a1",
    "xe",
    "a2",
    "xl",
    "a3",
    "a4",
    "x1",
    "square",
    "x2r1",
    "x3",
    "cl",
    "xn",
    "r2",
    "x4",
    "product",
    "parts",
    "sums",
    "r3",
    "c1b1",
    "r4",
    "c2b2",
    "rows",
    "c3b3",
    "cn",
    "c4",
    "fourth",
    "next",
)
SHORT = {"a_row": (4, 4), "a_col": (4, 4), "x_col": (4, 4), "s_row": (2, 2), "s_col": (4, 4), "sum": (4, 4)}


def reach(d, p):
    return 4 if d == p else 3


def hops(short, g, d, p):
    return min(short[d == p], reach(d, p)) if g else reach(d, p)


def events(short):
    return [(g, d, s, p) for g, d in RINGS for p in range(PARTS) for s in range(1, hops(short, g, d, p) + 1)]


def far(short):
    return [(d, s, p) for s in range(1, 5) for d in (0, 1) for p in range(PARTS) if hops(short, 1, d, p) < s <= reach(d, p)]


def sign(d):
    return 1 if d == 0 else -1


def wrap(v):
    return lax.rem(v + 16, 8)


def copies():
    count = {name: len(events(short)) + len(far(short)) for name, short in SHORT.items()}
    return sum(count.values()) + 5 * PARTS + 2 + 8 + 1


def piece(ref, p):
    return ref.at[pl.ds(p * (B // PARTS), B // PARTS)]


def halves(v):
    hi = v.astype(BF)
    return hi, (v - hi.astype(F32)).astype(BF)


def dot(a, b):
    return jnp.dot(a, b, preferred_element_type=F32)


def dot_t(a, b):
    return lax.dot_general(a, b, (((1,), (1,)), ((), ())), preferred_element_type=F32)


def kernel(a_ref, x_ref, q_ref, n_ref, f_ref, ar, ac, xc, sr, sc, part, swap, run, loan, last, s_own, t_own, acc2, acc1, p2, send, recv):
    row, col = lax.axis_index("row"), lax.axis_index("col")
    xh, y = row // 8, lax.rem(row, 8)
    z, xl, core = col // 4, lax.rem(col // 2, 2), lax.rem(col, 2)
    ids, groups = itertools.count(), itertools.count()

    y_dev = [(xh * 8 + wrap(y + sign(d)), col) for d in (0, 1)]
    z_dev = [(row, wrap(z + sign(d)) * 4 + xl * 2 + core) for d in (0, 1)]
    hi_dev = ((1 - xh) * 8 + y, col)
    lo_dev = (row, z * 4 + (1 - xl) * 2 + core)
    mate = (row, z * 4 + xl * 2 + (1 - core))

    barrier = pltpu.get_barrier_semaphore()
    across = [(row, wrap(z + sign(d)) * 4 + (1 - xl) * 2 + core) for d in (0, 1)]
    greeted = (*y_dev, *z_dev, *across, hi_dev, lo_dev, mate)
    for device in greeted:
        pl.semaphore_signal(barrier, inc=1, device_id=device, device_id_type=MESH)
    pl.semaphore_wait(barrier, len(greeted))

    def copy(k, src, dst, device, group=0):
        return pltpu.make_async_remote_copy(
            src_ref=src, dst_ref=dst, send_sem=send.at[group], recv_sem=recv.at[k], device_id=device, device_id_type=MESH
        )

    def start(group, k, src, dst, device):
        copy(k, src, dst, device, group).start()

    def arrived(k, dst):
        copy(k, dst, dst, mate).wait_recv()

    def all_sent(group, as_much):
        copy(0, as_much, as_much, mate, group).wait_send()

    class Panel:
        def __init__(self, buf, own, at, pos, devices, partner, mated, short):
            self.buf, self.own, self.at, self.pos = buf, own, at, pos
            self.devices, self.partner, self.mated, self.short = devices, partner, mated, short
            self.kx = [next(ids) for _ in range(PARTS)]
            self.group = next(groups)
            self.k = {e: next(ids) for e in events(short)}
            self.kf = {e: next(ids) for e in far(short)}
            self.km = next(ids) if mated else None

        def slot(self, g, d, s, p):
            return piece(self.buf.at[self.at(g, wrap(self.pos - sign(d) * s))], p)

        def to_mate(self, e, src=None):
            if self.mated:
                here = self.slot(*e)
                start(self.group, self.km, here if src is None else src, here, mate)

        def from_mate(self):
            arrived(self.km, self.buf.at[pl.ds(0, 16)])

        def all_sent(self):
            all_sent(self.group, self.buf.at[pl.ds(0, 31 if self.mated else 15)])

        def exchange(self):
            for p in range(PARTS):
                start(self.group, self.kx[p], piece(self.own, p), self.slot(0, 0, 0, p), self.partner)

        def forward(self, g, d, s, p):
            there = self.slot(g, d, s - 1, p)
            start(self.group, self.k[g, d, s, p], piece(self.own, p) if g == 0 and s == 1 else there, there, self.devices[d])

        def launch(self):
            for p in range(PARTS):
                for d in (0, 1):
                    self.forward(0, d, 1, p)
            for p in range(PARTS):
                self.to_mate((0, 0, 0, p), piece(self.own, p))

        def relaunch(self, p):
            arrived(self.kx[p], self.slot(1, 0, 0, p))
            for d in (0, 1):
                if hops(self.short, 1, d, p):
                    self.forward(1, d, 1, p)
            self.to_mate((1, 0, 0, p))

        def hop(self, g, d, s, p):
            e = (g, d, s, p)
            if e not in self.k:
                return
            here = self.slot(*e)
            arrived(self.k[e], here)
            if (g, d, s + 1, p) in self.k:
                self.forward(g, d, s + 1, p)
            if g == 0 and e[1:] in self.kf:
                start(self.group, self.kf[e[1:]], here, here, self.partner)
            self.to_mate(e)

        def step(self, s, g, p):
            if s == 1 and g == 0:
                self.relaunch(p)
            for d in (0, 1):
                self.hop(g, d, s, p)

        def finish(self, steps=(1, 2, 3, 4)):
            for e, k in self.kf.items():
                if e[1] in steps:
                    arrived(k, self.slot(1, *e))
                    self.to_mate((1, *e))

    def step(s, *panels):
        for g in (0, 1):
            for p in range(PARTS):
                for panel in panels:
                    panel.step(s, g, p)

    def row_at(g, p):
        lo = xl if g == 0 else 1 - xl
        return p * 4 + lo * 2 + core

    def col_at(g, p):
        return (xh if g == 0 else 1 - xh) * 8 + p

    def row_panel(buf, own, short):
        return Panel(buf, own, row_at, z, z_dev, lo_dev, True, short)

    def col_panel(buf, own, short):
        return Panel(buf, own, col_at, y, y_dev, hi_dev, False, short)

    def clear():
        acc2[...] = jnp.zeros_like(acc2)
        acc1[...] = jnp.zeros_like(acc1)

    def terms(left, right, first, count):
        def body(i, carry):
            here = wrap(y + i + first)
            lh, ll = halves(jnp.concatenate([left[2 * here + j] for j in (0, 1, 16, 17)], axis=1))
            rh, rl = halves(jnp.concatenate([right[here + j] for j in (0, 8)], axis=0))
            acc2[...] += dot(lh, jnp.concatenate([rh, rl], axis=1))
            acc1[...] += dot(ll, rh)
            return carry

        lax.fori_loop(0, count, body, 0)

    def value():
        return acc2[:, :H] + acc2[:, H:] + acc1[...]

    a_row, a_col = row_panel(ar, a_ref, SHORT["a_row"]), col_panel(ac, a_ref, SHORT["a_col"])
    s_row, s_col = row_panel(sr, s_own, SHORT["s_row"]), col_panel(sc, s_own, SHORT["s_col"])
    x_col = col_panel(xc, x_ref, SHORT["x_col"])

    def begin():
        a_col.launch()
        a_row.launch()
        a_col.exchange()
        a_row.exchange()
        ac[row] = a_ref[...]
        ar[col] = a_ref[...]
        xc[row] = x_ref[...]

    def square():
        a_row.finish()
        a_col.finish()
        a_row.from_mate()
        clear()
        terms(ar, ac, 0, 8)
        s_own[...] = value()
        s_row.launch()
        s_row.exchange()
        s_col.exchange()
        sr[col] = s_own[...]
        sc[row] = s_own[...]

    def near(left, right):
        clear()
        terms(left, right, -3, 7)

    def product():
        x_col.finish()
        terms(ar, xc, 4, 1)
        hi, lo = halves(value())
        p2[...] = jnp.concatenate([hi, lo], axis=1)

    order = (4, 3, 5, 2, 6, 1, 7, 0)
    kn = {o: next(ids) for o in order}
    g_part, g_sum = next(groups), next(groups)

    def part_of(o):
        zz = wrap(z + o)
        for l in (0, 1):
            bh, bl = halves(ac[2 * zz + l])
            both = dot_t(p2[...], jnp.concatenate([bh, bh], axis=1)) + dot_t(p2[:, :H], bl)
            part[0, zz, l] = both[:, :H]
            part[1, zz, l] = both[:, H:]
        start(g_part, kn[o], part.at[1 - core, zz], swap.at[zz], mate)

    short = SHORT["sum"]
    runs, lent = events(short), far(short)
    kr = {e: next(ids) for e in runs}
    kl = {e: next(ids) for e in lent}
    have = set()

    def share(g, d, s, p):
        zz = wrap(z + sign(d) * s)
        o = sign(d) * s % 8
        if o not in have:
            have.add(o)
            arrived(kn[o], swap.at[zz])
        l = xl if g == 0 else 1 - xl
        return piece(part.at[core, zz, l], p), piece(swap.at[zz, l], p)

    def lend(d, s, p):
        mine, theirs = share(1, d, s, p)
        mine[...] += theirs[...]
        start(g_sum, kl[d, s, p], mine, loan.at[lent.index((d, s, p))], lo_dev)

    def added(value, g, d, s, p):
        mine, theirs = share(g, d, s, p)
        value = mine[...] + theirs[...] if value is None else value + (mine[...] + theirs[...])
        if g == 0 and (d, s, p) in kl:
            here = loan.at[lent.index((d, s, p))]
            arrived(kl[d, s, p], here)
            value = value + here[...]
        return value

    def relay(g, d, p, s):
        n = hops(short, g, d, p)
        if not 1 <= s <= n:
            return
        if s == n:
            here = share(g, d, s, p)[0]
            here[...] = added(None, g, d, s, p)
        else:
            e = (g, d, n - s, p)
            here = run.at[runs.index(e)]
            arrived(kr[e], here)
            here[...] = added(here[...], g, d, s, p)
        e = (g, d, n - s + 1, p)
        there = across[d] if g == 1 and s == 1 else z_dev[d]
        start(g_sum, kr[e], here, run.at[runs.index(e)], there)

    def parts():
        for o in order[:3]:
            part_of(o)
        for d, s, p in reversed(lent):
            lend(d, s, p)
        for o in order[3:]:
            part_of(o)

    k_last = next(ids)

    def sums():
        advance([("b", 0)])
        for p in range(PARTS):
            mine, theirs = share(1, 0, 0, p)
            mine[...] += theirs[...]
        start(g_sum, k_last, part.at[core, z, 1 - xl], last, lo_dev)

    def fourth():
        s_col.finish()
        terms(sr, sc, 4, 1)
        f_ref[...] = value()

    def next_state():
        arrived(k_last, last)
        n_ref[...] = q_ref[...] + last[...]
        for p in range(PARTS):
            here = piece(n_ref, p)
            here[...] = added(here[...], 0, 0, 0, p)
            for g in (1, 0):
                for d in (0, 1):
                    e = (g, d, hops(short, g, d, p), p)
                    arrived(kr[e], run.at[runs.index(e)])
                    here[...] += run[runs.index(e)]

    def rows_done():
        s_row.finish()
        s_row.from_mate()

    todo = {
        "begin": begin,
        "square": square,
        "product": product,
        "parts": parts,
        "sums": sums,
        "fourth": fourth,
        "next": next_state,
        "rows": rows_done,
        "xe": x_col.exchange,
        "xl": x_col.launch,
        "cl": s_col.launch,
        "xn": lambda: near(ar, xc),
        "cn": lambda: near(sr, sc),
    }
    panels = {"a": (a_col, a_row), "x": (x_col,), "r": (s_row,), "c": (s_col,)}

    def advance(pairs):
        for g in (0, 1):
            for p in range(PARTS):
                for who, i in pairs:
                    for panel in panels.get(who, ()):
                        panel.step(i, g, p)
                    for d in (0, 1) if who == "b" else ():
                        relay(1 - g, d, p, hops(short, 1 - g, d, p) - i)

    for name in ORDER:
        if name in todo:
            todo.pop(name)()
        else:
            advance([(name[j], int(name[j + 1])) for j in range(0, len(name), 2)])
    for panel in (a_row, a_col, x_col, s_row, s_col):
        panel.all_sent()
    all_sent(g_part, swap.at[...])
    all_sent(g_sum, ar.at[pl.ds(0, 15)])
    assert not todo
    assert next(ids) == copies()


def on_device(operator, state, source):
    block = pltpu.VMEM((B, H), F32)
    vmem = pl.BlockSpec(memory_space=pltpu.VMEM)

    def blocks(*lead):
        return pltpu.VMEM((*lead, B, H), F32)

    return pl.pallas_call(
        kernel,
        out_shape=(block, block),
        in_specs=[vmem] * 3,
        out_specs=(vmem, vmem),
        scratch_shapes=[
            blocks(32),
            blocks(16),
            blocks(16),
            blocks(32),
            blocks(16),
            blocks(2, 8, 2),
            blocks(8, 2),
            pltpu.VMEM((len(events(SHORT["sum"])), B // PARTS, H), F32),
            pltpu.VMEM((max(1, len(far(SHORT["sum"]))), B // PARTS, H), F32),
            blocks(),
            blocks(),
            blocks(),
            pltpu.VMEM((B, B), F32),
            blocks(),
            pltpu.VMEM((B, B), BF),
            pltpu.SemaphoreType.DMA((7,)),
            pltpu.SemaphoreType.DMA((copies(),)),
        ],
        compiler_params=pltpu.CompilerParams(collective_id=0, has_side_effects=True, vmem_limit_bytes=56 << 20),
        name="smith",
    )(operator, state, source)


def solution(mesh):
    spec = P("row", "col")
    return jax.shard_map(on_device, mesh=mesh, in_specs=(spec, spec, spec), out_specs=(spec, spec), check_vma=False)
```
